32 devices in a mesh: kt: 4 (over z), ks: 8 (over y, x, core).
Axes of the slice: x: 2, y: 2, z: 4, core: 2. Of those that a mesh axis runs over, the one named last changes fastest.
Arguments:
- val_target: bfloat16 [8, 32, 512], P('kt', None, 'ks'), may hold values from -6 to 6
- cond_target: bfloat16 [8, 64, 512], P('kt', None, 'ks'), may hold values from -0.046875 to 0.046875
- val_source: bfloat16 [32, 32, 512], P('ks', None, 'kt'), may hold values from -6 to 6
- cond_source: bfloat16 [32, 64, 512], P('ks', None, 'kt'), may hold values from -0.125 to 0.125
- trial_vectors: bfloat16 [32, 16, 2048], P('ks', 'kt'), may hold values from -6 to 6
- screened: bfloat16 [512, 512, 512], P(None, ('kt', 'ks')), may hold values from -0.25 to 0.25
- pair_momentum: int32 [8, 32], replicated, may hold values from 0 to 511
Outputs:
- kernel_out: float32 [8, 16, 2048], P('kt', 'ks')
The draws below stay inside these ranges and needn't reach their ends.
All inputs are finite; a program needn't handle non-finite values.
Results may differ from the reference program's by a relative error of at most 0.019.
Values may be sent and summed in bfloat16 or wider, within the bound.
A program may use at most 128 MiB of HBM per device.

```python
import jax
import jax.numpy as jnp
from jax import lax

NAUX = 512
NV = 32
NC = 64
NVEC = 16
NQ = 512
NKT = 8
NKS = 32


def plant(drawn, own_key, low, top_value):
    spot = [jax.random.randint(jax.random.fold_in(own_key, axis), (), 0, length) for axis, length in enumerate(drawn.shape)]
    longest = drawn.shape.index(max(drawn.shape))
    next_to = spot[:longest] + [(spot[longest] + 1) % drawn.shape[longest]] + spot[longest + 1:]
    return drawn.at[tuple(spot)].set(low).at[tuple(next_to)].set(top_value)


def block_levels(rng, shape, cuts, least, high):
    def one(axis_at, parts):
        heights = jax.random.uniform(jax.random.fold_in(jax.random.fold_in(rng, 6), axis_at), (parts,), jnp.float32, least / len(cuts), high / len(cuts))
        return jnp.repeat(jnp.exp(heights), shape[axis_at] // parts).reshape((-1,) + (1,) * (len(shape) - axis_at - 1))

    gain = one(*cuts[0])
    for cut in cuts[1:]:
        gain = gain * one(*cut)
    return gain


def bell_draw(rng, extent, width, reach, pieces=(), kind=jnp.bfloat16):
    factor_of = block_levels(rng, extent, pieces, -0.22, 0.18) if pieces else 1.0
    drawn = jax.random.normal(rng, extent, jnp.float32) * width * factor_of
    return jnp.minimum(jnp.maximum(drawn, -reach), reach).astype(kind)


def setup_inputs(seed: int = 0) -> dict:
    key_list = jax.random.split(jax.random.key(seed), 8)
    return {
        "val_target": bell_draw(key_list[0], (NKT, NV, NAUX), 1.0, 6.0, ((0, 4), (2, 8))),
        "cond_target": bell_draw(key_list[1], (NKT, NC, NAUX), (NAUX * NKS) ** -0.5, 0.046875, ((0, 4), (2, 8))),
        "val_source": bell_draw(key_list[2], (NKS, NV, NAUX), 1.0, 6.0, ((0, 8), (2, 4))),
        "cond_source": bell_draw(key_list[3], (NKS, NC, NAUX), (NC * NV) ** -0.5, 0.125, ((0, 8), (2, 4))),
        "trial_vectors": bell_draw(key_list[4], (NKS, NVEC, NV * NC), 1.0, 6.0, ((0, 8), (1, 4))),
        "screened": bell_draw(key_list[5], (NQ, NAUX, NAUX), NAUX ** -0.5, 0.25, ((1, 32),)),
        "pair_momentum": plant(jax.random.randint(key_list[6], (NKT, NKS), 0, NQ), jax.random.fold_in(key_list[6], 1), 0, NQ - 1).astype(jnp.int32),
    }


def reference(val_target, cond_target, val_source, cond_source, trial_vectors, screened, pair_momentum):
    highest = lax.Precision.HIGHEST
    trial_four = trial_vectors.reshape(NKS, NVEC, NV, NC).astype(jnp.float32)
    dressed = jnp.einsum("snwc,scq->snwq", trial_four, cond_source.astype(jnp.float32), precision=highest)
    dressed = dressed.astype(jnp.bfloat16).astype(jnp.float32)

    def one_target(index):
        momentum = pair_momentum[index]
        kernel_mats = screened[momentum].astype(jnp.float32)
        target_val = val_target[index].astype(jnp.float32)
        pair_prod = (target_val[None, :, None, :] * val_source.astype(jnp.float32)[:, None, :, :]).astype(jnp.bfloat16)
        kernels = jnp.einsum("svwp,spq->svwq", pair_prod.astype(jnp.float32), kernel_mats, precision=highest)
        kernels = kernels.astype(jnp.bfloat16).astype(jnp.float32)
        reduced = jnp.einsum("svwq,snwq->vnq", kernels, dressed, precision=highest)
        reduced = reduced.astype(jnp.bfloat16).astype(jnp.float32)
        result = jnp.einsum("vnq,cq->nvc", reduced, cond_target[index].astype(jnp.float32), precision=highest)
        return result.reshape(NVEC, NV * NC)

    return lax.map(one_target, jnp.arange(NKT, dtype=jnp.int32))
```

```python
import functools

import jax
import jax.numpy as jnp
from jax import lax
from jax.experimental import pallas as pl
from jax.experimental.pallas import tpu as pltpu
from jax.sharding import PartitionSpec as P


def general(val_target, cond_target, val_source, cond_source, trial_vectors, screened, pair_momentum):
    tgt_val, tgt_cond = (
        lax.all_gather(val_target, "ks", axis=2, tiled=True),
        lax.all_gather(cond_target, "ks", axis=2, tiled=True),
    )
    src_val, src_cond, vectors = (
        lax.all_gather(val_source, "kt", axis=2, tiled=True),
        lax.all_gather(cond_source, "kt", axis=2, tiled=True),
        lax.all_gather(trial_vectors, "kt", axis=1, tiled=True),
    )
    count_kt = lax.axis_size("kt")
    count_ks = lax.axis_size("ks")
    tgt_count = tgt_val.shape[0]
    src_count = src_val.shape[0]
    pair_count = tgt_count * src_count
    width = screened.shape[2]
    val_bands = tgt_val.shape[1]
    cond_bands = tgt_cond.shape[1]
    vec_count = vectors.shape[1]
    table = pair_momentum.reshape(count_kt, tgt_count, count_ks, src_count)
    table = table.transpose(1, 3, 0, 2).reshape(pair_count, count_kt * count_ks)
    outgoing = screened[table]
    arrived = lax.all_to_all(outgoing, ("kt", "ks"), split_axis=1, concat_axis=1, tiled=True)
    pair_mats = arrived.reshape(tgt_count, src_count, width, width)
    trial_four = vectors.reshape(src_count, vec_count, val_bands, cond_bands)
    dressed = jnp.einsum(
        "snwc,scq->snwq", trial_four, src_cond, preferred_element_type=jnp.float32
    ).astype(jnp.bfloat16)
    pair_prod = (
        tgt_val.astype(jnp.float32)[:, None, :, None, :]
        * src_val.astype(jnp.float32)[None, :, None, :, :]
    ).astype(jnp.bfloat16)
    kernels = jnp.einsum(
        "tsvwp,tspq->tsvwq", pair_prod, pair_mats, preferred_element_type=jnp.float32
    ).astype(jnp.bfloat16)
    reduced = jnp.einsum(
        "tsvwq,snwq->tvnq", kernels, dressed, preferred_element_type=jnp.float32
    ).astype(jnp.bfloat16)
    partial_out = jnp.einsum(
        "tvnq,tcq->tnvc", reduced, tgt_cond, preferred_element_type=jnp.float32
    )
    partial_out = partial_out.reshape(tgt_count, vec_count, val_bands * cond_bands)
    return lax.psum_scatter(
        partial_out.astype(jnp.bfloat16), "ks", scatter_dimension=1, tiled=True
    ).astype(jnp.float32)


MESH = pl.DeviceIdType.MESH
VMEM = pl.BlockSpec(memory_space=pltpu.VMEM)


def remote(src, dst, send, recv, kt, ks):
    return pltpu.make_async_remote_copy(
        src_ref=src, dst_ref=dst, send_sem=send, recv_sem=recv, device_id=(kt, ks), device_id_type=MESH
    )


def greet(peers):
    barrier = pltpu.get_barrier_semaphore()
    for kt, ks in peers:
        pl.semaphore_signal(barrier, inc=1, device_id=(kt, ks), device_id_type=MESH)
    pl.semaphore_wait(barrier, len(peers))


def gather_kernel(nz, ns, block, vsx, vtx, out, vsg, vtg,
                  zs, zr, xs, xr, ys, yr, as_, ar, bs, br, ps, pr, vss, vsr, vts, vtr, ls):
    z, k = lax.axis_index("kt"), lax.axis_index("ks")
    core = lax.rem(k, 2)
    side = lax.rem(k // 2, 2)
    kx = k + 2 - 4 * side
    ky = lax.rem(k + 4, ns)
    kd = lax.rem(kx + 4, ns)
    kp = k + 1 - 2 * core
    half = block.shape[0] // 2
    first, second = pl.ds(0, half), pl.ds(half, half)
    zpeer = [lax.rem(z + j, nz) for j in range(nz)]
    speer = [lax.rem(k + j, ns) for j in range(ns)]
    greet([(zpeer[j], k) for j in range(1, nz)] + [(z, speer[j]) for j in range(1, ns)])

    slot = lambda zz, kk: out.at[zz * ns + kk]
    started = []

    def go(copy):
        copy.start()
        started.append(copy)

    def arrived(dst, recv):
        remote(dst, dst, recv, recv, z, kp).wait_recv()

    def partner(index, src, zz, kk):
        go(remote(src, slot(zz, kk), ps.at[index], pr.at[index], z, kp))

    for j in (1, nz - 1, *range(2, nz - 1)):
        go(remote(block, slot(z, k), zs.at[j], zr.at[nz - j], zpeer[j], k))
    go(remote(block, slot(z, k), xs.at[0], xr.at[0], z, kx))
    go(remote(block, slot(z, k), ys.at[0], yr.at[0], z, ky))
    partner(0, block, z, k)
    for j in range(1, ns):
        go(remote(vsx.at[speer[j]], vsg.at[k], vss.at[j], vsr.at[j], z, speer[j]))
        go(remote(vtx, vtg.at[k], vts.at[j], vtr.at[j], z, speer[j]))
    own = [
        pltpu.make_async_copy(block, slot(z, k), ls.at[0]),
        pltpu.make_async_copy(vsx.at[k], vsg.at[k], ls.at[1]),
        pltpu.make_async_copy(vtx, vtg.at[k], ls.at[2]),
    ]
    for copy in own:
        copy.start()

    order = [0, 1, nz - 1, *range(2, nz - 1)]

    def relay(j):
        zz = zpeer[j]
        arrived(slot(zz, kx), xr.at[j])
        go(remote(slot(zz, kx).at[first], slot(zz, kx).at[first], as_.at[j], ar.at[j], z, ky))
        partner(nz + j, slot(zz, kx), zz, kx)
        arrived(slot(zz, ky), yr.at[j])
        go(remote(slot(zz, ky).at[second], slot(zz, ky).at[second], bs.at[j], br.at[j], z, kx))
        partner(2 * nz + j, slot(zz, ky), zz, ky)

    def corner(j):
        zz = zpeer[j]
        arrived(slot(zz, kd).at[first], ar.at[j])
        arrived(slot(zz, kd).at[second], br.at[j])
        partner(3 * nz + j, slot(zz, kd), zz, kd)

    for place, j in enumerate(order):
        if place:
            zz = zpeer[j]
            arrived(slot(zz, k), zr.at[j])
            go(remote(slot(zz, k), slot(zz, k), xs.at[j], xr.at[j], z, kx))
            go(remote(slot(zz, k), slot(zz, k), ys.at[j], yr.at[j], z, ky))
            partner(j, slot(zz, k), zz, k)
            relay(order[place - 1])
        if place > 1:
            corner(order[place - 2])
    relay(order[-1])
    corner(order[-2])
    corner(order[-1])

    other = [kp, kx + 1 - 2 * core, lax.rem(kp + 4, ns), lax.rem(kx + 5 - 2 * core, ns)]
    for j in range(nz):
        for piece in range(4):
            arrived(slot(zpeer[j], other[piece]), pr.at[piece * nz + j])
    for j in range(1, ns):
        arrived(vsg.at[speer[ns - j]], vsr.at[j])
        arrived(vtg.at[speer[ns - j]], vtr.at[j])
    for copy in own:
        copy.wait()
    for copy in started:
        copy.wait_send()


def contract_kernel(nz, ns, nt, nsl, table, screened, gathered, vsg, out, wbuf, wide, mbuf, abuf, sem):
    pairs, rows, width = wbuf.shape
    src = ns * nsl
    tgt = nz * nt
    nvec = mbuf.shape[1] // rows
    lanes = 128
    halves = nvec // nz // 2

    def fetch(i, carry):
        pltpu.make_async_copy(screened.at[table[i]], wbuf.at[i], sem).start()
        return carry

    lax.fori_loop(0, pairs, fetch, 0)

    depth = vsg.shape[2] // nsl
    shape = (nsl * rows, nsl * depth)
    picked = lax.broadcasted_iota(jnp.int32, shape, 0) // rows == lax.broadcasted_iota(jnp.int32, shape, 1) // depth
    low = lax.broadcasted_iota(jnp.int32, (rows, lanes), 1) < lanes // 2
    trial_rows = halves * nsl * depth
    cond = lanes // 2

    def build(b, carry):
        left = jnp.concatenate([vsg[b].astype(jnp.float32)] * nsl, axis=0)
        left = jnp.where(picked, left, 0.0).astype(jnp.bfloat16)
        right = jnp.concatenate(
            [gathered[z * ns + b, h * nsl * depth:(h + 1) * nsl * depth, :] for z in range(nz) for h in range(halves)],
            axis=1,
        )
        folded = jnp.dot(left, right, preferred_element_type=jnp.float32)
        for s in range(nsl):
            parts = []
            for j in range(nvec // 2):
                piece = folded[s * rows:(s + 1) * rows, j * lanes:(j + 1) * lanes]
                parts += [jnp.where(low, piece, 0.0), jnp.where(low, 0.0, piece)]
            left_s = jnp.concatenate(parts, axis=0).astype(jnp.bfloat16)
            at = trial_rows + s * cond
            cond_s = jnp.concatenate([gathered[z * ns + b, at:at + cond, :] for z in range(nz)], axis=1)
            right_s = jnp.concatenate([cond_s, cond_s], axis=0)
            mbuf[b * nsl + s] = jnp.dot(left_s, right_s, preferred_element_type=jnp.float32)
        return carry

    lax.fori_loop(0, ns, build, 0)
    pltpu.make_async_copy(wbuf, wbuf, sem).wait()

    def widen(i, carry):
        wide[i] = wbuf[i].astype(jnp.float32)
        return carry

    lax.fori_loop(0, pairs, widen, 0, unroll=4)

    group = 4
    rblocks, qblocks = rows // 8, width // lanes

    def tile(i, carry):
        q = pl.ds(pl.multiple_of(lax.rem(i, qblocks) * lanes, lanes), lanes)
        rest = i // qblocks
        r = lax.rem(rest, rblocks) * 8
        n0 = (rest // rblocks) * group
        wrow = pl.ds(pl.multiple_of(r, 8), 8)
        mrow = [pl.ds(pl.multiple_of((n0 + g) * rows + r, 8), 8) for g in range(group)]

        def step(s, total):
            m = [mbuf[s, mrow[g], q] for g in range(group)]
            new = []
            for t in range(tgt):
                w = wide[t * src + s, wrow, q]
                new += [total[t * group + g] + w * m[g] for g in range(group)]
            return tuple(new)

        total = lax.fori_loop(0, src, step, tuple(jnp.zeros((8, lanes), jnp.float32) for _ in range(tgt * group)), unroll=2)
        for t in range(tgt):
            for g in range(group):
                abuf[t, mrow[g], q] = total[t * group + g]
        return carry

    lax.fori_loop(0, (nvec // group) * rblocks * qblocks, tile, 0)

    lowc = lax.broadcasted_iota(jnp.int32, (nvec * rows, lanes), 1) < lanes // 2
    at = trial_rows + nsl * cond
    for z in range(nz):
        right = jnp.concatenate([gathered[z * ns + b, at:, :] for b in range(ns)], axis=0)
        pair = [jnp.dot(abuf[z * nt + t].astype(jnp.bfloat16), right, preferred_element_type=jnp.float32) for t in range(nt)]
        out[z] = jnp.where(lowc, pair[0], pair[1]).astype(jnp.bfloat16)


def finish_kernel(nz, ns, sent, vtg, out, got, ss, rs, ls):
    z, k = lax.axis_index("kt"), lax.axis_index("ks")
    me = z * ns + k
    count = nz * ns
    barrier = pltpu.get_barrier_semaphore()

    def hello(j, carry):
        peer = lax.rem(me + j, count)
        pl.semaphore_signal(barrier, inc=1, device_id=(peer // ns, lax.rem(peer, ns)), device_id_type=MESH)
        return carry

    lax.fori_loop(1, count, hello, 0)
    pl.semaphore_wait(barrier, count - 1)

    def copy(j):
        peer = lax.rem(me + j, count)
        return remote(sent.at[peer], got.at[me], ss.at[j], rs.at[j], peer // ns, lax.rem(peer, ns))

    def go(j, carry):
        copy(j).start()
        return carry

    lax.fori_loop(1, count, go, 0)
    own = pltpu.make_async_copy(sent.at[me], got.at[me], ls)
    own.start()
    own.wait()

    def finish(j, carry):
        copy(j).wait_send()
        giver = got.at[lax.rem(me + count - j, count)]
        remote(giver, giver, ss.at[j], rs.at[j], z, k).wait_recv()
        return carry

    lax.fori_loop(1, count, finish, 0)
    nloc, both, bands = out.shape[0], out.shape[1], out.shape[2]
    rows = got.shape[1] // nloc
    left = jnp.concatenate([vtg[b] for b in range(ns)], axis=1)
    for n in range(nloc):
        right = jnp.concatenate([got[i, n * rows:(n + 1) * rows, :] for i in range(count)], axis=0)
        out[n] = jnp.dot(left, right, preferred_element_type=jnp.float32)


def local(val_target, cond_target, val_source, cond_source, trial_vectors, screened, pair_momentum):
    nz, ns = lax.axis_size("kt"), lax.axis_size("ks")
    nt, bands, pk = val_target.shape
    nc = cond_target.shape[1]
    nsl, _, pz = val_source.shape
    nv = trial_vectors.shape[1]
    rows, width = screened.shape[1:]
    nvec = nv * nz
    bf16, f32 = jnp.bfloat16, jnp.float32
    trial = trial_vectors.reshape(nsl, nv // 2, 2, bands, nc).transpose(1, 0, 3, 2, 4).reshape(-1, 2 * nc)
    block = jnp.concatenate(
        [trial, cond_source.reshape(nsl * nc, pz), cond_target.transpose(2, 0, 1).reshape(pk, nt * nc)], axis=0
    )
    vsx = val_source.reshape(nsl, bands, ns, rows).transpose(2, 3, 0, 1).reshape(ns, rows, nsl * bands)
    vtx = val_target.reshape(nt * bands, pk)
    dma = pltpu.SemaphoreType.DMA
    gathered, vsg, vtg = pl.pallas_call(
        functools.partial(gather_kernel, nz, ns),
        out_shape=(
            jax.ShapeDtypeStruct((nz * ns, *block.shape), bf16),
            jax.ShapeDtypeStruct(vsx.shape, bf16),
            jax.ShapeDtypeStruct((ns, *vtx.shape), bf16),
        ),
        in_specs=[VMEM] * 3,
        out_specs=(VMEM,) * 3,
        scratch_shapes=[dma((nz,))] * 10 + [dma((4 * nz,))] * 2 + [dma((ns,))] * 4 + [dma((3,))],
        compiler_params=pltpu.CompilerParams(collective_id=0, has_side_effects=True),
        name="gather",
    )(block, vsx, vtx)
    pairs = pair_momentum.size
    held = pl.pallas_call(
        functools.partial(contract_kernel, nz, ns, nt, nsl),
        out_shape=jax.ShapeDtypeStruct((nz, nvec * rows, nt * nc), bf16),
        in_specs=[
            pl.BlockSpec(memory_space=pltpu.SMEM),
            pl.BlockSpec(memory_space=pl.ANY),
            VMEM,
            VMEM,
        ],
        out_specs=VMEM,
        scratch_shapes=[
            pltpu.VMEM((pairs, rows, width), bf16),
            pltpu.VMEM((pairs, rows, width), f32),
            pltpu.VMEM((ns * nsl, nvec * rows, width), f32),
            pltpu.VMEM((nz * nt, nvec * rows, width), f32),
            dma,
        ],
        compiler_params=pltpu.CompilerParams(vmem_limit_bytes=56 * 2**20),
        name="contract",
    )(pair_momentum.reshape(-1), screened, gathered, vsg)
    nloc = nvec // ns
    sent = held.reshape(nz * ns, nloc * rows, nt * nc)
    wide = pl.pallas_call(
        functools.partial(finish_kernel, nz, ns),
        out_shape=jax.ShapeDtypeStruct((nloc, nt * bands, nt * nc), f32),
        in_specs=[VMEM] * 2,
        out_specs=VMEM,
        scratch_shapes=[pltpu.VMEM(sent.shape, bf16), dma((nz * ns,)), dma((nz * ns,)), dma],
        compiler_params=pltpu.CompilerParams(collective_id=1, has_side_effects=True),
        name="finish",
    )(sent, vtg)
    wide = wide.reshape(nloc, nt, bands, nt, nc)
    result = jnp.stack([wide[:, t, :, t, :] for t in range(nt)], axis=0)
    return result.reshape(nt, nloc, bands * nc)


def fits(mesh, args):
    val_target, cond_target, val_source, cond_source, trial_vectors, screened, pair_momentum = args
    nz, ns = mesh.shape["kt"], mesh.shape["ks"]
    aux = val_target.shape[2]
    nt, nvec, nc = val_target.shape[0] // nz, trial_vectors.shape[1], cond_target.shape[1]
    rows = aux // (nz * ns)
    return (
        ns == 8 and nz >= 3 and nt == 2 and 2 * nc == 128 and aux // nz == 128 and rows == 16
        and nvec % (2 * nz) == 0 and nvec % ns == 0 and pair_momentum.size <= 256
    )


def solution(mesh):
    in_specs = (
        P("kt", None, "ks"),
        P("kt", None, "ks"),
        P("ks", None, "kt"),
        P("ks", None, "kt"),
        P("ks", "kt", None),
        P(None, ("kt", "ks"), None),
        P(),
    )
    out_specs = P("kt", "ks", None)

    def whole(*args):
        body = local if fits(mesh, args) else general
        return jax.shard_map(body, mesh=mesh, in_specs=in_specs, out_specs=out_specs, check_vma=False)(*args)

    return whole
```

```python
import functools

import jax
import jax.numpy as jnp
from jax import lax
from jax.experimental import pallas as pl
from jax.experimental.pallas import tpu as pltpu
from jax.sharding import PartitionSpec as P


def general(val_target, cond_target, val_source, cond_source, trial_vectors, screened, pair_momentum):
    tgt_val, tgt_cond = (
        lax.all_gather(val_target, "ks", axis=2, tiled=True),
        lax.all_gather(cond_target, "ks", axis=2, tiled=True),
    )
    src_val, src_cond, vectors = (
        lax.all_gather(val_source, "kt", axis=2, tiled=True),
        lax.all_gather(cond_source, "kt", axis=2, tiled=True),
        lax.all_gather(trial_vectors, "kt", axis=1, tiled=True),
    )
    count_kt = lax.axis_size("kt")
    count_ks = lax.axis_size("ks")
    tgt_count = tgt_val.shape[0]
    src_count = src_val.shape[0]
    pair_count = tgt_count * src_count
    width = screened.shape[2]
    val_bands = tgt_val.shape[1]
    cond_bands = tgt_cond.shape[1]
    vec_count = vectors.shape[1]
    table = pair_momentum.reshape(count_kt, tgt_count, count_ks, src_count)
    table = table.transpose(1, 3, 0, 2).reshape(pair_count, count_kt * count_ks)
    outgoing = screened[table]
    arrived = lax.all_to_all(outgoing, ("kt", "ks"), split_axis=1, concat_axis=1, tiled=True)
    pair_mats = arrived.reshape(tgt_count, src_count, width, width)
    trial_four = vectors.reshape(src_count, vec_count, val_bands, cond_bands)
    dressed = jnp.einsum(
        "snwc,scq->snwq", trial_four, src_cond, preferred_element_type=jnp.float32
    ).astype(jnp.bfloat16)
    pair_prod = (
        tgt_val.astype(jnp.float32)[:, None, :, None, :]
        * src_val.astype(jnp.float32)[None, :, None, :, :]
    ).astype(jnp.bfloat16)
    kernels = jnp.einsum(
        "tsvwp,tspq->tsvwq", pair_prod, pair_mats, preferred_element_type=jnp.float32
    ).astype(jnp.bfloat16)
    reduced = jnp.einsum(
        "tsvwq,snwq->tvnq", kernels, dressed, preferred_element_type=jnp.float32
    ).astype(jnp.bfloat16)
    partial_out = jnp.einsum(
        "tvnq,tcq->tnvc", reduced, tgt_cond, preferred_element_type=jnp.float32
    )
    partial_out = partial_out.reshape(tgt_count, vec_count, val_bands * cond_bands)
    return lax.psum_scatter(
        partial_out.astype(jnp.bfloat16), "ks", scatter_dimension=1, tiled=True
    ).astype(jnp.float32)


MESH = pl.DeviceIdType.MESH
VMEM = pl.BlockSpec(memory_space=pltpu.VMEM)


def remote(src, dst, send, recv, kt, ks):
    return pltpu.make_async_remote_copy(
        src_ref=src, dst_ref=dst, send_sem=send, recv_sem=recv, device_id=(kt, ks), device_id_type=MESH
    )


def fused_kernel(nz, ns, nt, nsl, table, screened, block, vsx, vtx, result,
                 out, vsg, vtg, slab, wide, mbuf, abuf, sent, got,
                 zs, zr, xs, xr, ys, yr, as_, ar, bs, br, ps, pr, vss, vsr, vts, vtr, fs, fr, ls):
    z, k = lax.axis_index("kt"), lax.axis_index("ks")
    core = lax.rem(k, 2)
    side = lax.rem(k // 2, 2)
    kx = k + 2 - 4 * side
    ky = lax.rem(k + 4, ns)
    kd = lax.rem(kx + 4, ns)
    kp = k + 1 - 2 * core
    other = [kp, kx + 1 - 2 * core, lax.rem(kp + 4, ns), lax.rem(kx + 5 - 2 * core, ns)]
    half = block.shape[0] // 2
    first, second = pl.ds(0, half), pl.ds(half, half)
    zpeer = [lax.rem(z + j, nz) for j in range(nz)]
    speer = [lax.rem(k + j, ns) for j in range(ns)]
    me = z * ns + k
    count = nz * ns

    load = pltpu.make_async_copy(screened, slab, ls.at[3])
    load.start()
    own = [
        pltpu.make_async_copy(block, out.at[me], ls.at[0]),
        pltpu.make_async_copy(vsx.at[k], vsg.at[k], ls.at[1]),
        pltpu.make_async_copy(vtx, vtg.at[k], ls.at[2]),
    ]
    for copy in own:
        copy.start()

    barrier = pltpu.get_barrier_semaphore()

    def hello(j, carry):
        peer = lax.rem(me + j, count)
        pl.semaphore_signal(barrier, inc=1, device_id=(peer // ns, lax.rem(peer, ns)), device_id_type=MESH)
        return carry

    lax.fori_loop(1, count, hello, 0)
    pl.semaphore_wait(barrier, count - 1)

    slot = lambda zz, kk: out.at[zz * ns + kk]
    started = []

    def go(copy):
        copy.start()
        started.append(copy)

    def arrived(dst, recv):
        remote(dst, dst, recv, recv, z, kp).wait_recv()

    def partner(index, src, zz, kk):
        go(remote(src, slot(zz, kk), ps.at[index], pr.at[index], z, kp))

    for j in range(1, ns):
        go(remote(vsx.at[speer[j]], vsg.at[k], vss.at[j], vsr.at[j], z, speer[j]))
    for j in (1, nz - 1, *range(2, nz - 1)):
        go(remote(block, slot(z, k), zs.at[j], zr.at[nz - j], zpeer[j], k))
    go(remote(block, slot(z, k), xs.at[0], xr.at[0], z, kx))
    go(remote(block, slot(z, k), ys.at[0], yr.at[0], z, ky))
    partner(0, block, z, k)
    for j in range(1, ns):
        go(remote(vtx, vtg.at[k], vts.at[j], vtr.at[j], z, speer[j]))

    order = [0, 1, nz - 1, *range(2, nz - 1)]

    def spread(j):
        zz = zpeer[j]
        arrived(slot(zz, k), zr.at[j])
        go(remote(slot(zz, k), slot(zz, k), xs.at[j], xr.at[j], z, kx))
        go(remote(slot(zz, k), slot(zz, k), ys.at[j], yr.at[j], z, ky))
        partner(j, slot(zz, k), zz, k)

    def relay(j):
        zz = zpeer[j]
        arrived(slot(zz, kx), xr.at[j])
        go(remote(slot(zz, kx).at[first], slot(zz, kx).at[first], as_.at[j], ar.at[j], z, ky))
        partner(nz + j, slot(zz, kx), zz, kx)
        arrived(slot(zz, ky), yr.at[j])
        go(remote(slot(zz, ky).at[second], slot(zz, ky).at[second], bs.at[j], br.at[j], z, kx))
        partner(2 * nz + j, slot(zz, ky), zz, ky)

    def corner(j):
        zz = zpeer[j]
        arrived(slot(zz, kd).at[first], ar.at[j])
        arrived(slot(zz, kd).at[second], br.at[j])
        partner(3 * nz + j, slot(zz, kd), zz, kd)

    def passed(piece):
        for j in range(nz):
            arrived(slot(zpeer[j], other[piece]), pr.at[piece * nz + j])

    rows, width = slab.shape[1:]
    tgt = nz * nt
    nvec = mbuf.shape[1] // rows
    lanes = 128
    halves = nvec // nz // 2
    depth = vsg.shape[2] // nsl
    shape = (nsl * rows, nsl * depth)
    picked = lax.broadcasted_iota(jnp.int32, shape, 0) // rows == lax.broadcasted_iota(jnp.int32, shape, 1) // depth
    trial_rows = halves * nsl * depth
    cond = lanes // 2
    group = 4
    rblocks, qblocks = rows // 8, width // lanes

    def compute(b, fresh=False):
        low = lax.broadcasted_iota(jnp.int32, (rows, lanes), 1) < lanes // 2
        left = jnp.concatenate([vsg[b].astype(jnp.float32)] * nsl, axis=0)
        left = jnp.where(picked, left, 0.0).astype(jnp.bfloat16)
        right = jnp.concatenate(
            [out[zz * ns + b, h * nsl * depth:(h + 1) * nsl * depth, :] for zz in range(nz) for h in range(halves)],
            axis=1,
        )
        folded = jnp.dot(left, right, preferred_element_type=jnp.float32)
        for s in range(nsl):
            parts = []
            for j in range(nvec // 2):
                piece = folded[s * rows:(s + 1) * rows, j * lanes:(j + 1) * lanes]
                parts += [jnp.where(low, piece, 0.0), jnp.where(low, 0.0, piece)]
            left_s = jnp.concatenate(parts, axis=0).astype(jnp.bfloat16)
            at = trial_rows + s * cond
            cond_s = jnp.concatenate([out[zz * ns + b, at:at + cond, :] for zz in range(nz)], axis=1)
            right_s = jnp.concatenate([cond_s, cond_s], axis=0)
            mbuf[s] = jnp.dot(left_s, right_s, preferred_element_type=jnp.float32)

        def widen(t, carry):
            for s in range(nsl):
                wide[t * nsl + s] = slab[table[t, b * nsl + s]].astype(jnp.float32)
            return carry

        lax.fori_loop(0, tgt, widen, 0)

        def tile(i, carry):
            q = pl.ds(pl.multiple_of(lax.rem(i, qblocks) * lanes, lanes), lanes)
            rest = i // qblocks
            r = lax.rem(rest, rblocks) * 8
            n0 = (rest // rblocks) * group
            wrow = pl.ds(pl.multiple_of(r, 8), 8)
            mrow = [pl.ds(pl.multiple_of((n0 + g) * rows + r, 8), 8) for g in range(group)]
            total = {}
            for s in range(nsl):
                m = [mbuf[s, mrow[g], q] for g in range(group)]
                for t in range(tgt):
                    w = wide[t * nsl + s, wrow, q]
                    for g in range(group):
                        term = w * m[g]
                        total[t, g] = term if s == 0 else total[t, g] + term
            for t in range(tgt):
                for g in range(group):
                    value = total[t, g] if fresh else abuf[t, mrow[g], q] + total[t, g]
                    abuf[t, mrow[g], q] = value
            return carry

        lax.fori_loop(0, (nvec // group) * rblocks * qblocks, tile, 0)

    spread(order[1])
    relay(order[0])
    spread(order[2])
    relay(order[1])
    corner(order[0])
    for j in order[3:]:
        spread(j)
    for copy in own:
        copy.wait()
    for j in range(1, ns):
        arrived(vsg.at[speer[ns - j]], vsr.at[j])
    load.wait()
    compute(k, True)
    for place in range(2, nz):
        relay(order[place])
        corner(order[place - 1])
        if place == 2:
            passed(0)
            compute(kp)
    compute(kx)
    corner(order[-1])
    passed(1)
    passed(2)

    def later(i, carry):
        one = i // 2
        sx = lax.rem(i + 1, 2) * one + (1 - one) * lax.rem(i, 2)
        sy = (1 - one) + one * lax.rem(i, 2)
        kc = k + one * (1 - 2 * core)
        compute(lax.rem(kc + sx * (2 - 4 * side) + 4 * sy, ns))
        return carry

    lax.fori_loop(0, 4, later, 0)
    passed(3)
    compute(other[3])

    lowc = lax.broadcasted_iota(jnp.int32, (nvec * rows, lanes), 1) < lanes // 2
    at = trial_rows + nsl * cond
    chunk = sent.shape[1] // ns

    def deal(dz, dk):
        zz, kk = lax.rem(z + dz, nz), lax.rem(k + dk, ns)
        src = sent.at[zz, pl.ds(pl.multiple_of(kk * chunk, chunk), chunk)]
        return remote(src, got.at[me], fs.at[dz, dk], fr.at[dz, dk], zz, kk)

    def emit(i, carry):
        dz = lax.rem(i + 1, nz)
        zz = lax.rem(z + dz, nz)
        right = jnp.concatenate([out[zz * ns + b, at:, :] for b in range(ns)], axis=0)
        pair = [jnp.dot(abuf[zz * nt + t].astype(jnp.bfloat16), right, preferred_element_type=jnp.float32) for t in range(nt)]
        sent[zz] = jnp.where(lowc, pair[0], pair[1]).astype(jnp.bfloat16)

        def push(dk, carry):
            deal(dz, dk).start()
            return carry

        lax.fori_loop((i + 1) // nz, ns, push, 0)
        return carry

    lax.fori_loop(0, nz, emit, 0)
    mine = pltpu.make_async_copy(sent.at[z, pl.ds(pl.multiple_of(k * chunk, chunk), chunk)], got.at[me], ls.at[4])
    mine.start()
    mine.wait()
    for copy in started:
        copy.wait_send()
    for j in range(1, ns):
        arrived(vtg.at[speer[ns - j]], vtr.at[j])

    def settle(i, carry):
        dz, dk = i // ns, lax.rem(i, ns)
        deal(dz, dk).wait_send()
        giver = got.at[lax.rem(z + nz - dz, nz) * ns + lax.rem(k + ns - dk, ns)]
        remote(giver, giver, fs.at[dz, dk], fr.at[dz, dk], z, kp).wait_recv()
        return carry

    lax.fori_loop(1, count, settle, 0)
    left = jnp.concatenate([vtg[b] for b in range(ns)], axis=1)
    for n in range(result.shape[0]):
        right = jnp.concatenate([got[i, n * rows:(n + 1) * rows, :] for i in range(count)], axis=0)
        result[n] = jnp.dot(left, right, preferred_element_type=jnp.float32)


def local(val_target, cond_target, val_source, cond_source, trial_vectors, screened, pair_momentum):
    nz, ns = lax.axis_size("kt"), lax.axis_size("ks")
    nt, bands, pk = val_target.shape
    nc = cond_target.shape[1]
    nsl, _, pz = val_source.shape
    nv = trial_vectors.shape[1]
    rows, width = screened.shape[1:]
    nvec = nv * nz
    nloc = nvec // ns
    bf16, f32 = jnp.bfloat16, jnp.float32
    trial = trial_vectors.reshape(nsl, nv // 2, 2, bands, nc).transpose(1, 0, 3, 2, 4).reshape(-1, 2 * nc)
    block = jnp.concatenate(
        [trial, cond_source.reshape(nsl * nc, pz), cond_target.transpose(2, 0, 1).reshape(pk, nt * nc)], axis=0
    )
    vsx = val_source.reshape(nsl, bands, ns, rows).transpose(2, 3, 0, 1).reshape(ns, rows, nsl * bands)
    vtx = val_target.reshape(nt * bands, pk)
    dma = pltpu.SemaphoreType.DMA
    wide = pl.pallas_call(
        functools.partial(fused_kernel, nz, ns, nt, nsl),
        out_shape=jax.ShapeDtypeStruct((nloc, nt * bands, nt * nc), f32),
        in_specs=[pl.BlockSpec(memory_space=pltpu.SMEM), pl.BlockSpec(memory_space=pl.ANY)] + [VMEM] * 3,
        out_specs=VMEM,
        scratch_shapes=[
            pltpu.VMEM((nz * ns, *block.shape), bf16),
            pltpu.VMEM(vsx.shape, bf16),
            pltpu.VMEM((ns, *vtx.shape), bf16),
            pltpu.VMEM(screened.shape, bf16),
            pltpu.VMEM((nz * nt * nsl, rows, width), f32),
            pltpu.VMEM((nsl, nvec * rows, width), f32),
            pltpu.VMEM((nz * nt, nvec * rows, width), f32),
            pltpu.VMEM((nz, nvec * rows, nt * nc), bf16),
            pltpu.VMEM((nz * ns, nloc * rows, nt * nc), bf16),
        ]
        + [dma((nz,))] * 10 + [dma((4 * nz,))] * 2 + [dma((ns,))] * 4 + [dma((nz, ns))] * 2 + [dma((5,))],
        compiler_params=pltpu.CompilerParams(
            collective_id=0, has_side_effects=True, vmem_limit_bytes=48 * 2**20
        ),
        name="fused",
    )(pair_momentum, screened, block, vsx, vtx)
    wide = wide.reshape(nloc, nt, bands, nt, nc)
    result = jnp.stack([wide[:, t, :, t, :] for t in range(nt)], axis=0)
    return result.reshape(nt, nloc, bands * nc)


def fits(mesh, args):
    val_target, cond_target, val_source, cond_source, trial_vectors, screened, pair_momentum = args
    nz, ns = mesh.shape["kt"], mesh.shape["ks"]
    aux = val_target.shape[2]
    nt, nvec, nc = val_target.shape[0] // nz, trial_vectors.shape[1], cond_target.shape[1]
    rows = aux // (nz * ns)
    return (
        ns == 8 and nz >= 3 and nt == 2 and 2 * nc == 128 and aux // nz == 128 and rows == 16
        and nvec % (2 * nz) == 0 and nvec % ns == 0 and pair_momentum.size <= 256
    )


def solution(mesh):
    in_specs = (
        P("kt", None, "ks"),
        P("kt", None, "ks"),
        P("ks", None, "kt"),
        P("ks", None, "kt"),
        P("ks", "kt", None),
        P(None, ("kt", "ks"), None),
        P(),
    )
    out_specs = P("kt", "ks", None)

    def whole(*args):
        body = local if fits(mesh, args) else general
        return jax.shard_map(body, mesh=mesh, in_specs=in_specs, out_specs=out_specs, check_vma=False)(*args)

    return whole
```

```python
import functools

import jax
import jax.numpy as jnp
from jax import lax
from jax.experimental import pallas as pl
from jax.experimental.pallas import tpu as pltpu
from jax.sharding import PartitionSpec as P


def general(val_target, cond_target, val_source, cond_source, trial_vectors, screened, pair_momentum):
    tgt_val, tgt_cond = (
        lax.all_gather(val_target, "ks", axis=2, tiled=True),
        lax.all_gather(cond_target, "ks", axis=2, tiled=True),
    )
    src_val, src_cond, vectors = (
        lax.all_gather(val_source, "kt", axis=2, tiled=True),
        lax.all_gather(cond_source, "kt", axis=2, tiled=True),
        lax.all_gather(trial_vectors, "kt", axis=1, tiled=True),
    )
    count_kt = lax.axis_size("kt")
    count_ks = lax.axis_size("ks")
    tgt_count = tgt_val.shape[0]
    src_count = src_val.shape[0]
    pair_count = tgt_count * src_count
    width = screened.shape[2]
    val_bands = tgt_val.shape[1]
    cond_bands = tgt_cond.shape[1]
    vec_count = vectors.shape[1]
    table = pair_momentum.reshape(count_kt, tgt_count, count_ks, src_count)
    table = table.transpose(1, 3, 0, 2).reshape(pair_count, count_kt * count_ks)
    outgoing = screened[table]
    arrived = lax.all_to_all(outgoing, ("kt", "ks"), split_axis=1, concat_axis=1, tiled=True)
    pair_mats = arrived.reshape(tgt_count, src_count, width, width)
    trial_four = vectors.reshape(src_count, vec_count, val_bands, cond_bands)
    dressed = jnp.einsum(
        "snwc,scq->snwq", trial_four, src_cond, preferred_element_type=jnp.float32
    ).astype(jnp.bfloat16)
    pair_prod = (
        tgt_val.astype(jnp.float32)[:, None, :, None, :]
        * src_val.astype(jnp.float32)[None, :, None, :, :]
    ).astype(jnp.bfloat16)
    kernels = jnp.einsum(
        "tsvwp,tspq->tsvwq", pair_prod, pair_mats, preferred_element_type=jnp.float32
    ).astype(jnp.bfloat16)
    reduced = jnp.einsum(
        "tsvwq,snwq->tvnq", kernels, dressed, preferred_element_type=jnp.float32
    ).astype(jnp.bfloat16)
    partial_out = jnp.einsum(
        "tvnq,tcq->tnvc", reduced, tgt_cond, preferred_element_type=jnp.float32
    )
    partial_out = partial_out.reshape(tgt_count, vec_count, val_bands * cond_bands)
    return lax.psum_scatter(
        partial_out.astype(jnp.bfloat16), "ks", scatter_dimension=1, tiled=True
    ).astype(jnp.float32)


MESH = pl.DeviceIdType.MESH
VMEM = pl.BlockSpec(memory_space=pltpu.VMEM)


def remote(src, dst, send, recv, kt, ks):
    return pltpu.make_async_remote_copy(
        src_ref=src, dst_ref=dst, send_sem=send, recv_sem=recv, device_id=(kt, ks), device_id_type=MESH
    )


def fused_kernel(nz, ns, nt, nsl, table, screened, block, vsx, vtx, result,
                 out, vsg, vtg, slab, wide, mbuf, abuf, sent, got,
                 zs, zr, xs, xr, ys, yr, as_, ar, bs, br, ps, pr, vss, vsr, vts, vtr, fs, fr, ls):
    z, k = lax.axis_index("kt"), lax.axis_index("ks")
    core = lax.rem(k, 2)
    side = lax.rem(k // 2, 2)
    kx = k + 2 - 4 * side
    ky = lax.rem(k + 4, ns)
    kd = lax.rem(kx + 4, ns)
    kp = k + 1 - 2 * core
    other = [kp, kx + 1 - 2 * core, lax.rem(kp + 4, ns), lax.rem(kx + 5 - 2 * core, ns)]
    half = block.shape[0] // 2
    first, second = pl.ds(0, half), pl.ds(half, half)
    zpeer = [lax.rem(z + j, nz) for j in range(nz)]
    speer = [lax.rem(k + j, ns) for j in range(ns)]
    me = z * ns + k
    count = nz * ns

    load = pltpu.make_async_copy(screened, slab, ls.at[3])
    load.start()
    own = [
        pltpu.make_async_copy(block, out.at[me], ls.at[0]),
        pltpu.make_async_copy(vsx.at[k], vsg.at[k], ls.at[1]),
        pltpu.make_async_copy(vtx, vtg.at[k], ls.at[2]),
    ]
    for copy in own:
        copy.start()

    barrier = pltpu.get_barrier_semaphore()

    def hello(j, carry):
        peer = lax.rem(me + j, count)
        pl.semaphore_signal(barrier, inc=1, device_id=(peer // ns, lax.rem(peer, ns)), device_id_type=MESH)
        return carry

    lax.fori_loop(1, count, hello, 0)
    pl.semaphore_wait(barrier, count - 1)

    slot = lambda zz, kk: out.at[zz * ns + kk]
    started = []

    def go(copy):
        copy.start()
        started.append(copy)

    def arrived(dst, recv):
        remote(dst, dst, recv, recv, z, kp).wait_recv()

    def partner(index, src, zz, kk):
        go(remote(src, slot(zz, kk), ps.at[index], pr.at[index], z, kp))

    for j in range(1, ns):
        go(remote(vsx.at[speer[j]], vsg.at[k], vss.at[j], vsr.at[j], z, speer[j]))
    for j in (1, nz - 1, *range(2, nz - 1)):
        go(remote(block, slot(z, k), zs.at[j], zr.at[nz - j], zpeer[j], k))
    go(remote(block, slot(z, k), xs.at[0], xr.at[0], z, kx))
    go(remote(block, slot(z, k), ys.at[0], yr.at[0], z, ky))
    partner(0, block, z, k)
    for j in range(1, ns):
        go(remote(vtx, vtg.at[k], vts.at[j], vtr.at[j], z, speer[j]))

    order = [0, 1, nz - 1, *range(2, nz - 1)]

    def spread(j):
        zz = zpeer[j]
        arrived(slot(zz, k), zr.at[j])
        go(remote(slot(zz, k), slot(zz, k), xs.at[j], xr.at[j], z, kx))
        go(remote(slot(zz, k), slot(zz, k), ys.at[j], yr.at[j], z, ky))
        partner(j, slot(zz, k), zz, k)

    def relay(j):
        zz = zpeer[j]
        arrived(slot(zz, kx), xr.at[j])
        go(remote(slot(zz, kx).at[first], slot(zz, kx).at[first], as_.at[j], ar.at[j], z, ky))
        partner(nz + j, slot(zz, kx), zz, kx)
        arrived(slot(zz, ky), yr.at[j])
        go(remote(slot(zz, ky).at[second], slot(zz, ky).at[second], bs.at[j], br.at[j], z, kx))
        partner(2 * nz + j, slot(zz, ky), zz, ky)

    def corner(j):
        zz = zpeer[j]
        arrived(slot(zz, kd).at[first], ar.at[j])
        arrived(slot(zz, kd).at[second], br.at[j])
        partner(3 * nz + j, slot(zz, kd), zz, kd)

    def passed(piece):
        for j in range(nz):
            arrived(slot(zpeer[j], other[piece]), pr.at[piece * nz + j])

    rows, width = slab.shape[1:]
    tgt = nz * nt
    nvec = mbuf.shape[1] // rows
    lanes = 128
    halves = nvec // nz // 2
    depth = vsg.shape[2] // nsl
    shape = (nsl * rows, nsl * depth)
    picked = lax.broadcasted_iota(jnp.int32, shape, 0) // rows == lax.broadcasted_iota(jnp.int32, shape, 1) // depth
    trial_rows = halves * nsl * depth
    cond = lanes // 2
    group = 4
    rblocks, qblocks = rows // 8, width // lanes

    def compute(b, fresh=False):
        low = lax.broadcasted_iota(jnp.int32, (rows, lanes), 1) < lanes // 2
        left = jnp.concatenate([vsg[b].astype(jnp.float32)] * nsl, axis=0)
        left = jnp.where(picked, left, 0.0).astype(jnp.bfloat16)
        right = jnp.concatenate(
            [out[zz * ns + b, h * nsl * depth:(h + 1) * nsl * depth, :] for zz in range(nz) for h in range(halves)],
            axis=1,
        )
        folded = jnp.dot(left, right, preferred_element_type=jnp.float32)
        for s in range(nsl):
            parts = []
            for j in range(nvec // 2):
                piece = folded[s * rows:(s + 1) * rows, j * lanes:(j + 1) * lanes]
                parts += [jnp.where(low, piece, 0.0), jnp.where(low, 0.0, piece)]
            left_s = jnp.concatenate(parts, axis=0).astype(jnp.bfloat16)
            at = trial_rows + s * cond
            cond_s = jnp.concatenate([out[zz * ns + b, at:at + cond, :] for zz in range(nz)], axis=1)
            right_s = jnp.concatenate([cond_s, cond_s], axis=0)
            mbuf[s] = jnp.dot(left_s, right_s, preferred_element_type=jnp.float32)

        def widen(t, carry):
            for s in range(nsl):
                wide[t * nsl + s] = slab[table[t, b * nsl + s]].astype(jnp.float32)
            return carry

        lax.fori_loop(0, tgt, widen, 0)

        def tile(i, carry):
            q = pl.ds(pl.multiple_of(lax.rem(i, qblocks) * lanes, lanes), lanes)
            rest = i // qblocks
            r = lax.rem(rest, rblocks) * 8
            n0 = (rest // rblocks) * group
            wrow = pl.ds(pl.multiple_of(r, 8), 8)
            mrow = [pl.ds(pl.multiple_of((n0 + g) * rows + r, 8), 8) for g in range(group)]
            total = {}
            for s in range(nsl):
                m = [mbuf[s, mrow[g], q] for g in range(group)]
                for t in range(tgt):
                    w = wide[t * nsl + s, wrow, q]
                    for g in range(group):
                        term = w * m[g]
                        total[t, g] = term if s == 0 else total[t, g] + term
            for t in range(tgt):
                for g in range(group):
                    value = total[t, g] if fresh else abuf[t, mrow[g], q] + total[t, g]
                    abuf[t, mrow[g], q] = value
            return carry

        lax.fori_loop(0, (nvec // group) * rblocks * qblocks, tile, 0)

    spread(order[1])
    relay(order[0])
    spread(order[2])
    relay(order[1])
    corner(order[0])
    for j in order[3:]:
        spread(j)
    for copy in own:
        copy.wait()
    for j in range(1, ns):
        arrived(vsg.at[speer[ns - j]], vsr.at[j])
    load.wait()
    compute(k, True)
    passed(0)
    compute(kp)
    relay(order[2])
    corner(order[1])
    for place in range(3, nz):
        relay(order[place])
    compute(kx)
    for place in range(2, nz - 1):
        corner(order[place])
    compute(ky)
    corner(order[-1])
    passed(1)
    passed(2)

    def later(i, carry):
        one = i // 2
        sx = lax.rem(i + 1, 2) * one + (1 - one) * lax.rem(i, 2)
        sy = (1 - one) + one * lax.rem(i, 2)
        kc = k + one * (1 - 2 * core)
        compute(lax.rem(kc + sx * (2 - 4 * side) + 4 * sy, ns))
        return carry

    lax.fori_loop(1, 4, later, 0)
    passed(3)
    compute(other[3])

    lowc = lax.broadcasted_iota(jnp.int32, (nvec * rows, lanes), 1) < lanes // 2
    at = trial_rows + nsl * cond
    chunk = sent.shape[1] // ns

    def deal(dz, dk):
        zz, kk = lax.rem(z + dz, nz), lax.rem(k + dk, ns)
        src = sent.at[zz, pl.ds(pl.multiple_of(kk * chunk, chunk), chunk)]
        return remote(src, got.at[me], fs.at[dz, dk], fr.at[dz, dk], zz, kk)

    def emit(i, carry):
        dz = lax.rem(i + 1, nz)
        zz = lax.rem(z + dz, nz)
        right = jnp.concatenate([out[zz * ns + b, at:, :] for b in range(ns)], axis=0)
        pair = [jnp.dot(abuf[zz * nt + t].astype(jnp.bfloat16), right, preferred_element_type=jnp.float32) for t in range(nt)]
        sent[zz] = jnp.where(lowc, pair[0], pair[1]).astype(jnp.bfloat16)

        def push(dk, carry):
            deal(dz, dk).start()
            return carry

        lax.fori_loop((i + 1) // nz, ns, push, 0)
        return carry

    lax.fori_loop(0, nz, emit, 0)
    mine = pltpu.make_async_copy(sent.at[z, pl.ds(pl.multiple_of(k * chunk, chunk), chunk)], got.at[me], ls.at[4])
    mine.start()
    mine.wait()
    for copy in started:
        copy.wait_send()
    for j in range(1, ns):
        arrived(vtg.at[speer[ns - j]], vtr.at[j])

    def settle(i, carry):
        dz, dk = i // ns, lax.rem(i, ns)
        deal(dz, dk).wait_send()
        giver = got.at[lax.rem(z + nz - dz, nz) * ns + lax.rem(k + ns - dk, ns)]
        remote(giver, giver, fs.at[dz, dk], fr.at[dz, dk], z, kp).wait_recv()
        return carry

    lax.fori_loop(1, count, settle, 0)
    left = jnp.concatenate([vtg[b] for b in range(ns)], axis=1)
    for n in range(result.shape[0]):
        right = jnp.concatenate([got[i, n * rows:(n + 1) * rows, :] for i in range(count)], axis=0)
        result[n] = jnp.dot(left, right, preferred_element_type=jnp.float32)


def local(val_target, cond_target, val_source, cond_source, trial_vectors, screened, pair_momentum):
    nz, ns = lax.axis_size("kt"), lax.axis_size("ks")
    nt, bands, pk = val_target.shape
    nc = cond_target.shape[1]
    nsl, _, pz = val_source.shape
    nv = trial_vectors.shape[1]
    rows, width = screened.shape[1:]
    nvec = nv * nz
    nloc = nvec // ns
    bf16, f32 = jnp.bfloat16, jnp.float32
    trial = trial_vectors.reshape(nsl, nv // 2, 2, bands, nc).transpose(1, 0, 3, 2, 4).reshape(-1, 2 * nc)
    block = jnp.concatenate(
        [trial, cond_source.reshape(nsl * nc, pz), cond_target.transpose(2, 0, 1).reshape(pk, nt * nc)], axis=0
    )
    vsx = val_source.reshape(nsl, bands, ns, rows).transpose(2, 3, 0, 1).reshape(ns, rows, nsl * bands)
    vtx = val_target.reshape(nt * bands, pk)
    dma = pltpu.SemaphoreType.DMA
    wide = pl.pallas_call(
        functools.partial(fused_kernel, nz, ns, nt, nsl),
        out_shape=jax.ShapeDtypeStruct((nloc, nt * bands, nt * nc), f32),
        in_specs=[pl.BlockSpec(memory_space=pltpu.SMEM), pl.BlockSpec(memory_space=pl.ANY)] + [VMEM] * 3,
        out_specs=VMEM,
        scratch_shapes=[
            pltpu.VMEM((nz * ns, *block.shape), bf16),
            pltpu.VMEM(vsx.shape, bf16),
            pltpu.VMEM((ns, *vtx.shape), bf16),
            pltpu.VMEM(screened.shape, bf16),
            pltpu.VMEM((nz * nt * nsl, rows, width), f32),
            pltpu.VMEM((nsl, nvec * rows, width), f32),
            pltpu.VMEM((nz * nt, nvec * rows, width), f32),
            pltpu.VMEM((nz, nvec * rows, nt * nc), bf16),
            pltpu.VMEM((nz * ns, nloc * rows, nt * nc), bf16),
        ]
        + [dma((nz,))] * 10 + [dma((4 * nz,))] * 2 + [dma((ns,))] * 4 + [dma((nz, ns))] * 2 + [dma((5,))],
        compiler_params=pltpu.CompilerParams(
            collective_id=0, has_side_effects=True, vmem_limit_bytes=48 * 2**20
        ),
        name="fused",
    )(pair_momentum, screened, block, vsx, vtx)
    wide = wide.reshape(nloc, nt, bands, nt, nc)
    result = jnp.stack([wide[:, t, :, t, :] for t in range(nt)], axis=0)
    return result.reshape(nt, nloc, bands * nc)


def fits(mesh, args):
    val_target, cond_target, val_source, cond_source, trial_vectors, screened, pair_momentum = args
    nz, ns = mesh.shape["kt"], mesh.shape["ks"]
    aux = val_target.shape[2]
    nt, nvec, nc = val_target.shape[0] // nz, trial_vectors.shape[1], cond_target.shape[1]
    rows = aux // (nz * ns)
    return (
        ns == 8 and nz >= 4 and nt == 2 and 2 * nc == 128 and aux // nz == 128 and rows == 16
        and nvec % (2 * nz) == 0 and nvec % ns == 0 and pair_momentum.size <= 256
    )


def solution(mesh):
    in_specs = (
        P("kt", None, "ks"),
        P("kt", None, "ks"),
        P("ks", None, "kt"),
        P("ks", None, "kt"),
        P("ks", "kt", None),
        P(None, ("kt", "ks"), None),
        P(),
    )
    out_specs = P("kt", "ks", None)

    def whole(*args):
        body = local if fits(mesh, args) else general
        return jax.shard_map(body, mesh=mesh, in_specs=in_specs, out_specs=out_specs, check_vma=False)(*args)

    return whole
```
